32 devices in a mesh: grp: 2 (over y), tok: 8 (over z, x), seq: 2 (over core).
Axes of the slice: x: 2, y: 2, z: 4, core: 2. Of those that a mesh axis runs over, the one named last changes fastest.
Arguments:
- pair_slab_input: bfloat16 [16, 128, 128], P(('grp', 'seq'), 'tok'), parts along dimension 0, may hold values from -6 to 6
- alignment_rows: bfloat16 [2048, 128, 64], P(('grp', 'seq'), 'tok'), parts along dimension 0, may hold values from -6 to 6
- alignment_row_mask: int32 [2048, 128], P(('grp', 'seq'), 'tok'), parts along dimension 0, may hold values 0 or 1
- residue: int32 [256], P(('grp', 'tok')), parts along dimension 0, may hold values from 0 to 95
- chain: int32 [256], P(('grp', 'tok')), parts along dimension 0, may hold values from 0 to 1
- template_key_mask: int32 [16, 128], P(('grp', 'seq')), parts along dimension 0, may hold values 0 or 1
- triangle_head_bias: bfloat16 [4, 256, 128], P(None, ('grp', 'tok')), parts along dimension 1, may hold values from -8 to 400
- pair_attention_gain: float32 [128], replicated, may hold values from 0.25 to 1.75
- query_gate_weight: bfloat16 [128, 256], replicated, may hold values from -0.5 to 0.5
- key_value_weight: bfloat16 [128, 256], replicated, may hold values from -0.5 to 0.5
- attention_output_weight: bfloat16 [128, 128], replicated, may hold values from -0.5 to 0.5
- relative_position_weight: bfloat16 [66, 128], replicated, may hold values from -6 to 6
- alignment_norm_gain: float32 [64], replicated, may hold values from 0.25 to 1.75
- left_factor_weight: bfloat16 [64, 32], replicated, may hold values from -0.75 to 0.75
- right_factor_weight: bfloat16 [64, 32], replicated, may hold values from -0.75 to 0.75
- outer_product_weight: bfloat16 [1024, 128], replicated, may hold values from -8 to 8
- outer_product_bias: float32 [128], replicated, may hold values from -4 to 4
- transition_gain: float32 [128], replicated, may hold values from 0.25 to 1.75
- transition_input_weight: bfloat16 [128, 1024], replicated, may hold values from -0.5 to 0.5
- transition_output_weight: bfloat16 [512, 128], replicated, may hold values from -0.25 to 0.25
Outputs:
- pair_output: bfloat16 [16, 128, 128], P(('grp', 'seq'), 'tok'), parts along dimension 0
The draws below stay inside these ranges and needn't reach their ends.
There are 2 independent parts, one for each index of `grp`. The reference program is written for one: setup_inputs(seed, part) draws one part's arguments, and reference() takes and returns one part's arrays. A program takes and returns all parts, laid end to end along the dimension named above; an argument that names none is the same for every part. Nothing has to cross between parts.
All inputs are finite; a program needn't handle non-finite values. No bound on the sum of `alignment_row_mask` or of `template_key_mask` on one device may be relied on, other than what follows from the above.
Results may differ from the reference program's by a relative error of at most 0.008.
Values may be sent and summed in bfloat16 or wider, within the bound.
No kernel may reach another device: no remote copies, remote signals or barrier semaphores. Data moves between devices by JAX's collectives and lax.ppermute only.
A program may use at most 64 MiB of HBM per device.

```python
import jax
import jax.numpy as jnp
from jax import lax

PAIR_DIM = 128
ALIGNMENT_WIDTH = 64
FACTOR_CHANNELS = 32
HEADS = 4
HEAD_DIM = 32
HIDDEN_DIM = 512
REL_MAX = 32
SLAB_ROW_COUNT = 8
ALIGNED_SEQUENCES = 1024
TOKEN_COUNT = 128
HEAD_WIDTH = 128
REL_BINS = 66


def draw_triangle_head_bias(key, part):
    base_key = jax.random.fold_in(jax.random.fold_in(key, 11), 0)
    array_shape = (HEADS, TOKEN_COUNT, TOKEN_COUNT)
    values = jnp.clip(2.0 * jax.random.normal(base_key, array_shape, jnp.float32), -8.0, 8.0)
    return values.astype(jnp.bfloat16)


def set_ends(values, own_key, least, largest):
    dims = values.shape
    place = [jax.random.randint(jax.random.fold_in(own_key, axis), (), 0, dims[axis]) for axis in range(len(dims))]
    values = values.at[tuple(place)].set(least)
    longest = dims.index(max(dims))
    place[longest] = (place[longest] + 1) % dims[longest]
    return values.at[tuple(place)].set(largest)


def block_levels(rng, dims, cuts, low, largest):
    level, own = 1.0, jax.random.fold_in(rng, 6)
    for axis_at, shards_of in cuts:
        steps = jnp.exp(jax.random.uniform(jax.random.fold_in(own, axis_at), (shards_of,), jnp.float32, low / len(cuts), largest / len(cuts)))
        level = level * jnp.repeat(steps, dims[axis_at] // shards_of).reshape([-1 if axis == axis_at else 1 for axis in range(len(dims))])
    return level


def bell_draw(rng, dims, spread, most, pieces=(), kind=jnp.bfloat16):
    loudness = block_levels(rng, dims, pieces, -0.22, 0.18) if pieces else 1.0
    entries = jax.random.normal(rng, dims, jnp.float32) * spread * loudness
    return jnp.minimum(jnp.maximum(entries, -most), most).astype(kind)


def setup_inputs(seed: int = 0, part: int = 0) -> dict:
    arg_keys = jax.random.split(jax.random.key(seed), 21)
    part_splits = jax.random.split(jax.random.fold_in(arg_keys[20], part), 21)
    return {
        "pair_slab_input": bell_draw(part_splits[0], (SLAB_ROW_COUNT, TOKEN_COUNT, PAIR_DIM), 1.0, 6.0, ((0, 2), (1, 8))),
        "alignment_rows": bell_draw(part_splits[1], (ALIGNED_SEQUENCES, TOKEN_COUNT, ALIGNMENT_WIDTH), 1.0, 6.0, ((0, 2), (1, 8))),
        "alignment_row_mask": set_ends((jax.random.randint(part_splits[2], (ALIGNED_SEQUENCES, TOKEN_COUNT), 0, 4) < 3).astype(jnp.int32), jax.random.fold_in(part_splits[2], 1), 0, 1),
        "residue": set_ends(jax.random.randint(part_splits[3], (TOKEN_COUNT,), 0, 96), jax.random.fold_in(part_splits[3], 1), 0, 95).astype(jnp.int32),
        "chain": set_ends(jax.random.randint(part_splits[4], (TOKEN_COUNT,), 0, 2), jax.random.fold_in(part_splits[4], 1), 0, 1).astype(jnp.int32),
        "template_key_mask": set_ends((jax.random.randint(part_splits[5], (SLAB_ROW_COUNT, TOKEN_COUNT), 0, 4) < 3).astype(jnp.int32), jax.random.fold_in(part_splits[5], 1), 0, 1),
        "triangle_head_bias": draw_triangle_head_bias(jax.random.fold_in(jax.random.fold_in(arg_keys[20], part), 71), part),
        "pair_attention_gain": jnp.clip(1.0 + 0.15 * jax.random.normal(arg_keys[7], (PAIR_DIM,), jnp.float32), 0.25, 1.75),
        "query_gate_weight": bell_draw(arg_keys[8], (PAIR_DIM, 2 * HEAD_WIDTH), PAIR_DIM ** -0.5, 0.5),
        "key_value_weight": bell_draw(arg_keys[9], (PAIR_DIM, 2 * HEAD_WIDTH), PAIR_DIM ** -0.5, 0.5),
        "attention_output_weight": bell_draw(arg_keys[10], (HEAD_WIDTH, PAIR_DIM), HEAD_WIDTH ** -0.5, 0.5),
        "relative_position_weight": bell_draw(arg_keys[11], (REL_BINS, PAIR_DIM), 1 ** -0.5, 6.0),
        "alignment_norm_gain": jnp.clip(1.0 + 0.15 * jax.random.normal(arg_keys[12], (ALIGNMENT_WIDTH,), jnp.float32), 0.25, 1.75),
        "left_factor_weight": bell_draw(arg_keys[13], (ALIGNMENT_WIDTH, FACTOR_CHANNELS), ALIGNMENT_WIDTH ** -0.5, 0.75),
        "right_factor_weight": bell_draw(arg_keys[14], (ALIGNMENT_WIDTH, FACTOR_CHANNELS), ALIGNMENT_WIDTH ** -0.5, 0.75),
        "outer_product_weight": bell_draw(arg_keys[15], (FACTOR_CHANNELS * FACTOR_CHANNELS, PAIR_DIM), (ALIGNED_SEQUENCES ** 0.5 / (0.75 * FACTOR_CHANNELS)), 8.0),
        "outer_product_bias": bell_draw(arg_keys[16], (PAIR_DIM,), 1.0, 4.0, (), jnp.float32),
        "transition_gain": jnp.clip(1.0 + 0.15 * jax.random.normal(arg_keys[17], (PAIR_DIM,), jnp.float32), 0.25, 1.75),
        "transition_input_weight": bell_draw(arg_keys[18], (PAIR_DIM, 2 * HIDDEN_DIM), PAIR_DIM ** -0.5, 0.5),
        "transition_output_weight": bell_draw(arg_keys[19], (HIDDEN_DIM, PAIR_DIM), HIDDEN_DIM ** -0.5, 0.25),
    }


EPS = 1e-05
MASKED = -1000000000.0

def apply_layer_norm(values, gain):
    mean = lax.optimization_barrier(jnp.mean(values, axis=-1, keepdims=True))
    centred = values - mean
    variance = lax.optimization_barrier(jnp.mean(centred * centred, axis=-1, keepdims=True))
    return centred * lax.rsqrt(variance + EPS) * gain

def reference(pair_slab_input, alignment_rows, alignment_row_mask, residue, chain, template_key_mask, triangle_head_bias, pair_attention_gain, query_gate_weight, key_value_weight, attention_output_weight, relative_position_weight, alignment_norm_gain, left_factor_weight, right_factor_weight, outer_product_weight, outer_product_bias, transition_gain, transition_input_weight, transition_output_weight):
    row_res = residue[:SLAB_ROW_COUNT]
    row_chain = chain[:SLAB_ROW_COUNT]
    offset = jnp.clip(row_res[:, None] - residue[None, :] + REL_MAX, 0, 2 * REL_MAX)
    rel_class = jnp.where(row_chain[:, None] == chain[None, :], offset, 2 * REL_MAX + 1).astype(jnp.int32)
    onehot = (rel_class[:, :, None] == jnp.arange(REL_BINS, dtype=jnp.int32)[None, None, :]).astype(jnp.bfloat16)
    relpos = jnp.dot(onehot.reshape(-1, REL_BINS), relative_position_weight, preferred_element_type=jnp.float32)
    pair_start = pair_slab_input.astype(jnp.float32) + relpos.reshape(SLAB_ROW_COUNT, TOKEN_COUNT, PAIR_DIM)
    pair_normed = apply_layer_norm(pair_start, pair_attention_gain).astype(jnp.bfloat16)
    bias_wide = triangle_head_bias.astype(jnp.float32)

    def attend_row(inputs):
        row_normed, row_mask = inputs
        query_gate = jnp.dot(row_normed, query_gate_weight, preferred_element_type=jnp.float32)
        query = query_gate[:, :HEAD_WIDTH].astype(jnp.bfloat16).reshape(TOKEN_COUNT, HEADS, HEAD_DIM)
        gate = jax.nn.sigmoid(query_gate[:, HEAD_WIDTH:])
        key_value = jnp.dot(row_normed, key_value_weight, preferred_element_type=jnp.float32).astype(jnp.bfloat16)
        key = key_value[:, :HEAD_WIDTH].reshape(TOKEN_COUNT, HEADS, HEAD_DIM)
        value = key_value[:, HEAD_WIDTH:].reshape(TOKEN_COUNT, HEADS, HEAD_DIM)
        logits = jnp.einsum('jhd,khd->hjk', query.astype(jnp.float32), key.astype(jnp.float32)) * HEAD_DIM ** (-0.5) + bias_wide
        logits = jnp.where(row_mask[None, None, :] == 1, logits, MASKED)
        peak = lax.optimization_barrier(jnp.max(logits, axis=-1, keepdims=True))
        expo = jnp.exp(logits - peak)
        total = lax.optimization_barrier(jnp.sum(expo, axis=-1))
        numer = jnp.einsum('hjk,khd->hjd', expo.astype(jnp.bfloat16).astype(jnp.float32), value.astype(jnp.float32))
        mixed = (numer / total[:, :, None]).transpose(1, 0, 2).reshape(TOKEN_COUNT, HEAD_WIDTH) * gate
        return jnp.dot(mixed.astype(jnp.bfloat16), attention_output_weight, preferred_element_type=jnp.float32)
    attn_update = lax.map(attend_row, (pair_normed, template_key_mask))
    pair_mid = pair_start + attn_update
    alignment_normed = apply_layer_norm(alignment_rows.astype(jnp.float32), alignment_norm_gain).astype(jnp.bfloat16)
    mask_as_float = alignment_row_mask.astype(jnp.float32)[:, :, None]
    left_factor = (mask_as_float[:, :SLAB_ROW_COUNT] * jnp.einsum('ijd,dy->ijy', alignment_normed[:, :SLAB_ROW_COUNT].astype(jnp.float32), left_factor_weight.astype(jnp.float32))).astype(jnp.bfloat16)
    right_factor = (mask_as_float * jnp.einsum('ijd,dy->ijy', alignment_normed.astype(jnp.float32), right_factor_weight.astype(jnp.float32))).astype(jnp.bfloat16)
    outer = jnp.einsum('sip,sjq->ijpq', left_factor.astype(jnp.float32), right_factor.astype(jnp.float32)).reshape(SLAB_ROW_COUNT, TOKEN_COUNT, FACTOR_CHANNELS * FACTOR_CHANNELS) / ALIGNED_SEQUENCES
    projected = jnp.dot(outer.reshape(-1, FACTOR_CHANNELS * FACTOR_CHANNELS), outer_product_weight.astype(jnp.float32), precision=lax.Precision.HIGHEST)
    pair_after = pair_mid + projected.reshape(SLAB_ROW_COUNT, TOKEN_COUNT, PAIR_DIM) + outer_product_bias
    trans_normed = apply_layer_norm(pair_after, transition_gain).astype(jnp.bfloat16).reshape(-1, PAIR_DIM)
    both = jnp.dot(trans_normed, transition_input_weight, preferred_element_type=jnp.float32)
    hidden = (jax.nn.silu(both[:, :HIDDEN_DIM]) * both[:, HIDDEN_DIM:]).astype(jnp.bfloat16)
    update = jnp.dot(hidden, transition_output_weight, preferred_element_type=jnp.float32).reshape(SLAB_ROW_COUNT, TOKEN_COUNT, PAIR_DIM)
    return (pair_after + update).astype(jnp.bfloat16)
```

```python
import functools

import jax
import jax.numpy as jnp
from jax import lax
from jax.experimental import pallas as pl
from jax.experimental.pallas import tpu as pltpu
from jax.sharding import PartitionSpec as P

HEADS = 4
REL_MAX = 32
EPS = 1e-05
MASKED = -1000000000.0
DIRECT_MAX = 8


F32 = jnp.float32
BF16 = jnp.bfloat16
VMEM = pl.BlockSpec(memory_space=pltpu.VMEM)
SMEM = pl.BlockSpec(memory_space=pltpu.SMEM)


def column_of(row, size):
    here = lax.broadcasted_iota(jnp.int32, (size, size), 0) == lax.broadcasted_iota(
        jnp.int32, (size, size), 1
    )
    return jnp.sum(jnp.where(here, row, 0.0), axis=1, keepdims=True)


def factor_of(rows, mask_row, gain_col, weight_t):
    values = rows.astype(F32)
    mean = jnp.mean(values, axis=0, keepdims=True)
    centred = values - mean
    variance = jnp.mean(centred * centred, axis=0, keepdims=True)
    normed = (centred * lax.rsqrt(variance + EPS) * gain_col).astype(BF16)
    factor = jnp.dot(weight_t, normed, preferred_element_type=F32)
    return (factor * mask_row.astype(F32)).astype(BF16)


def left_kernel(x_ref, mask_ref, gain_ref, weight_ref, pair_ref, res_ref, chain_ref, place_ref, far_ref, near_ref, payload_ref):
    rows_dev, tokens_dev, channels = pair_ref.shape
    factor_dim = weight_ref.shape[0]
    gain_col = column_of(gain_ref[...], gain_ref.shape[1])
    weight_t = weight_ref[...]
    seq = place_ref[1]
    for half, out_ref in ((1 - seq, far_ref), (seq, near_ref)):
        for i in range(rows_dev):
            token = half * rows_dev + i
            out_ref[pl.ds(i * factor_dim, factor_dim), :] = factor_of(
                x_ref[token], mask_ref[pl.ds(token, 1), :], gain_col, weight_t
            )
    for r in range(rows_dev):
        payload_ref[pl.ds(r * tokens_dev, tokens_dev), :] = pair_ref[r]
    lane = lax.broadcasted_iota(jnp.int32, (tokens_dev, channels), 1)
    res_col = column_of(res_ref[...].astype(F32), tokens_dev)
    chain_col = column_of(chain_ref[...].astype(F32), tokens_dev)
    payload_ref[pl.ds(rows_dev * tokens_dev, tokens_dev), :] = jnp.where(
        lane < channels // 2, res_col, chain_col
    ).astype(BF16)


def right_kernel(x_ref, mask_ref, gain_ref, weight_ref, out_ref):
    factor_dim = weight_ref.shape[0]
    gain_col = column_of(gain_ref[...], gain_ref.shape[1])
    weight_t = weight_ref[...]
    for token in range(x_ref.shape[0]):
        out_ref[pl.ds(token * factor_dim, factor_dim), :] = factor_of(
            x_ref[token], mask_ref[pl.ds(token, 1), :], gain_col, weight_t
        )


def norm_lanes(values, gain_row):
    mean = jnp.mean(values, axis=1, keepdims=True)
    centred = values - mean
    variance = jnp.mean(centred * centred, axis=1, keepdims=True)
    return (centred * lax.rsqrt(variance + EPS) * gain_row).astype(BF16)


def attention_kernel(split, *refs):
    (place_ref, mask_ref, bias_ref, gain_ref, qg_ref, kv_ref, out_w_ref, rel_ref, opb_ref), refs = refs[:9], refs[9:]
    pieces, (out_ref, start_ref, code_ref) = refs[:-3], refs[-3:]
    rows_dev, width = mask_ref.shape
    heads, tokens_dev, _ = bias_ref.shape
    channels = gain_ref.shape[1]
    head_width = out_w_ref.shape[0]
    head_dim = head_width // heads
    rel_bins = rel_ref.shape[0]
    block = (rows_dev + 1) * tokens_dev
    tok, seq = place_ref[0], place_ref[1]
    for k in range(width // tokens_dev):
        if split:
            piece, base, where = pieces[k], 0, jnp.bitwise_xor(tok, k) * tokens_dev
            where = pl.multiple_of(where, tokens_dev)
        else:
            piece, base, where = pieces[0], k * block, k * tokens_dev
        for r in range(rows_dev):
            start_ref[r, pl.ds(where, tokens_dev), :] = piece[
                pl.ds(base + r * tokens_dev, tokens_dev), :
            ].astype(F32)
        code_ref[pl.ds(where, tokens_dev), :] = piece[
            pl.ds(base + rows_dev * tokens_dev, tokens_dev), :
        ].astype(F32)
    codes = code_ref[...]
    key_res = codes[:, :1]
    key_chain = codes[:, channels - 1 :]
    gain_row = gain_ref[...]
    classes = lax.broadcasted_iota(jnp.int32, (width, rel_bins), 1).astype(F32)
    own = pl.ds(pl.multiple_of(tok * tokens_dev, tokens_dev), tokens_dev)
    keys, values = [], []
    for r in range(rows_dev):
        row_code = code_ref[pl.ds(seq * rows_dev + r, 1), :]
        offset = jnp.clip(row_code[:, :1] - key_res + REL_MAX, 0, 2 * REL_MAX)
        rel_class = jnp.where(row_code[:, channels - 1 :] == key_chain, offset, 2 * REL_MAX + 1)
        onehot = jnp.where(classes == rel_class, 1.0, 0.0).astype(BF16)
        start = start_ref[r] + jnp.dot(onehot, rel_ref[...], preferred_element_type=F32)
        start_ref[r] = start
        normed = norm_lanes(start, gain_row)
        key_value = jnp.dot(normed, kv_ref[...], preferred_element_type=F32).astype(BF16)
        keys.append(key_value[:, :head_width])
        values.append(key_value[:, head_width:])
    mine = jnp.concatenate([start_ref[r, own, :] for r in range(rows_dev)], axis=0)
    query_gate = jnp.dot(norm_lanes(mine, gain_row), qg_ref[...], preferred_element_type=F32)
    query = query_gate[:, :head_width]
    gate = jax.nn.sigmoid(query_gate[:, head_width:])
    stacked = heads * tokens_dev
    bias = bias_ref[...].astype(F32).reshape(stacked, width)
    head_of_row = lax.broadcasted_iota(jnp.int32, (stacked, head_width), 0) // tokens_dev
    head_of_lane = lax.broadcasted_iota(jnp.int32, (stacked, head_width), 1) // head_dim
    same_head = head_of_row == head_of_lane
    mixed = []
    for r in range(rows_dev):
        query_r = query[r * tokens_dev : (r + 1) * tokens_dev]
        wide = jnp.where(same_head, jnp.concatenate([query_r] * heads, axis=0), 0.0).astype(BF16)
        logits = lax.dot_general(
            wide, keys[r], (((1,), (1,)), ((), ())), preferred_element_type=F32
        )
        logits = logits * head_dim ** (-0.5) + bias
        logits = jnp.where(mask_ref[r : r + 1, :] == 1, logits, MASKED)
        expo = jnp.exp(logits - jnp.max(logits, axis=1, keepdims=True))
        total = jnp.sum(expo, axis=1, keepdims=True)
        numer = jnp.dot(expo.astype(BF16), values[r], preferred_element_type=F32)
        picked = jnp.where(same_head, numer / total, 0.0)
        mixed.append(
            sum(picked[h * tokens_dev : (h + 1) * tokens_dev] for h in range(heads))
        )
    attended = (jnp.concatenate(mixed, axis=0) * gate).astype(BF16)
    update = jnp.dot(attended, out_w_ref[...], preferred_element_type=F32)
    out_ref[...] = mine + update + opb_ref[...]


def project(left_t, right_t, weight, count, scratch, factor_dim):
    rows = left_t.shape[0] // factor_dim
    tokens = right_t.shape[0] // factor_dim
    lanes = rows * factor_dim
    scratch[...] = lax.dot_general(
        right_t, left_t, (((1,), (1,)), ((), ())), preferred_element_type=F32
    ) * (1.0 / count)
    segment = lax.broadcasted_iota(jnp.int32, (tokens, lanes), 1) // factor_dim
    groups = [[] for _ in range(rows)]
    for group in range(factor_dim // rows):
        level = [scratch[pl.ds(group * rows + a, tokens, stride=factor_dim), :] for a in range(rows)]
        step = 1
        while step < rows:
            upper = (segment & step) != 0
            for low in range(rows):
                if low & step:
                    continue
                one, two = level[low], level[low + step]
                level[low] = jnp.where(upper, pltpu.roll(two, step * factor_dim, 1), one)
                level[low + step] = jnp.where(
                    upper, two, pltpu.roll(one, lanes - step * factor_dim, 1)
                )
            step *= 2
        for r in range(rows):
            groups[r].append(level[r])
    outer = jnp.concatenate([jnp.concatenate(g, axis=1) for g in groups], axis=0)
    high = outer.astype(BF16)
    low = (outer - high.astype(F32)).astype(BF16)
    return jnp.dot(high, weight, preferred_element_type=F32) + jnp.dot(
        low, weight, preferred_element_type=F32
    )


def pick(flag, one_ref, two_ref):
    return jnp.where(flag != 0, two_ref[...], one_ref[...])


def far_kernel(count, factor_dim, flag_ref, left_ref, came_ref, right_ref, weight_ref, out_ref, scratch):
    left_t = pick(flag_ref[2], left_ref, came_ref)
    out_ref[...] = project(left_t, right_ref[...], weight_ref[...], count, scratch, factor_dim).astype(
        BF16
    )


def near_kernel(count, factor_dim, flag_ref, left_ref, came_ref, right_ref, weight_ref, mid_ref, other_ref, gain_ref, in_w_ref, out_w_ref, out_ref, scratch):
    left_t = pick(flag_ref[2], left_ref, came_ref)
    after = (
        mid_ref[...]
        + project(left_t, right_ref[...], weight_ref[...], count, scratch, factor_dim)
        + other_ref[...].astype(F32)
    )
    normed = norm_lanes(after, gain_ref[...])
    both = jnp.dot(normed, in_w_ref[...], preferred_element_type=F32)
    hidden_dim = out_w_ref.shape[0]
    up = both[:, :hidden_dim]
    hidden = (up * jax.nn.sigmoid(up) * both[:, hidden_dim:]).astype(BF16)
    update = jnp.dot(hidden, out_w_ref[...], preferred_element_type=F32)
    out_ref[...] = (after + update).astype(BF16)


def call(kernel, outs, specs, scratch=(), flops=0, **kw):
    one = not isinstance(outs, (list, tuple))
    return pl.pallas_call(
        kernel,
        out_shape=outs,
        in_specs=specs,
        out_specs=VMEM if one else [VMEM] * len(outs),
        scratch_shapes=scratch,
        cost_estimate=pl.CostEstimate(flops=flops, transcendentals=0, bytes_accessed=1 << 20),
        **kw,
    )


def swap(value, axis, bit, size):
    return lax.ppermute(value, axis, [(i, i ^ bit) for i in range(size)])


def on_device(
    pair_slab_input,
    alignment_rows,
    alignment_row_mask,
    residue,
    chain,
    template_key_mask,
    triangle_head_bias,
    pair_attention_gain,
    query_gate_weight,
    key_value_weight,
    attention_output_weight,
    relative_position_weight,
    alignment_norm_gain,
    left_factor_weight,
    right_factor_weight,
    outer_product_weight,
    outer_product_bias,
    transition_gain,
    transition_input_weight,
    transition_output_weight,
):
    rows_dev, tokens_dev, channels = pair_slab_input.shape
    sequences = alignment_rows.shape[0]
    factor_dim = left_factor_weight.shape[1]
    size = lax.axis_size("tok")
    seqs = lax.axis_size("seq")
    count = sequences * seqs
    width = template_key_mask.shape[1]
    slab = rows_dev * seqs
    tok, seq = lax.axis_index("tok"), lax.axis_index("seq")
    bits = [1 << k for k in range(size.bit_length() - 1)]
    tree = bits[:1] + bits[:0:-1]
    flag = jnp.stack([tok, seq, (tok & tree[-1]) // tree[-1]]).astype(jnp.int32)
    sds = jax.ShapeDtypeStruct

    rows_t = alignment_rows.transpose(1, 2, 0)
    mask_t = alignment_row_mask.T
    gain_row = alignment_norm_gain[None]
    half = sds((rows_dev * factor_dim, sequences), BF16)
    head_tokens = -(-slab // 8) * 8
    far, near, payload = call(
        left_kernel,
        [half, half, sds(((rows_dev + 1) * tokens_dev, channels), BF16)],
        [VMEM] * 7 + [SMEM],
        flops=1 << 28,
    )(
        rows_t[:head_tokens], mask_t[:head_tokens], gain_row, left_factor_weight.T, pair_slab_input, residue[None], chain[None], flag,
    )
    right_t = call(
        right_kernel,
        sds((tokens_dev * factor_dim, sequences), BF16),
        [VMEM] * 4,
        flops=1 << 29,
    )(rows_t, mask_t, gain_row, right_factor_weight.T)

    split = size <= DIRECT_MAX
    if split:
        pieces = [payload]
        for bit in bits:
            pieces = pieces + [swap(piece, "tok", bit, size) for piece in pieces]
    else:
        pieces = [lax.all_gather(payload, "tok", axis=0, tiled=True)]

    held = [far, near]
    came = held
    for stage, bit in enumerate(tree):
        if stage:
            took = (tok & tree[stage - 1]) != 0
            held = [jnp.where(took, b, a) for a, b in zip(held, came)]
        below = sum(tree[:stage])
        senders = [i for i in range(size) if i & ~below == 0 or not stage]
        pairs = sorted({(i, i ^ bit) for i in senders} | {(i ^ bit, i) for i in senders})
        came = [lax.ppermute(h, "tok", pairs) for h in held]

    mid = call(
        functools.partial(attention_kernel, split),
        sds((rows_dev * tokens_dev, channels), F32),
        [SMEM] + [VMEM] * (8 + len(pieces)),
        scratch=[
            pltpu.VMEM((rows_dev, width, channels), F32),
            pltpu.VMEM((width, channels), F32),
        ],
        flops=1 << 30,
    )(
        flag, template_key_mask, triangle_head_bias, pair_attention_gain[None], query_gate_weight, key_value_weight,
        attention_output_weight, relative_position_weight, outer_product_bias[None], *pieces,
    )

    weight = (
        outer_product_weight.reshape(factor_dim, factor_dim, channels)
        .transpose(1, 0, 2)
        .reshape(factor_dim * factor_dim, channels)
    )
    scratch = [pltpu.VMEM((tokens_dev * factor_dim, rows_dev * factor_dim), F32)]
    flat = (rows_dev * tokens_dev, channels)
    other = call(
        functools.partial(far_kernel, count, factor_dim),
        sds(flat, BF16),
        [SMEM] + [VMEM] * 4,
        scratch=scratch,
        flops=1 << 28,
    )(flag, held[0], came[0], right_t, weight)
    other = swap(other, "seq", 1, seqs)
    out = call(
        functools.partial(near_kernel, count, factor_dim),
        sds(flat, BF16),
        [SMEM] + [VMEM] * 9,
        scratch=scratch,
        flops=1 << 28,
    )(
        flag, held[1], came[1], right_t, weight, mid, other, transition_gain[None], transition_input_weight, transition_output_weight,
    )
    return out.reshape(rows_dev, tokens_dev, channels)


def solution(mesh):
    placed = (
        P(("grp", "seq"), "tok", None),
        P(("grp", "seq"), "tok", None),
        P(("grp", "seq"), "tok"),
        P(("grp", "tok")),
        P(("grp", "tok")),
        P(("grp", "seq"), None),
        P(None, ("grp", "tok"), None),
    ) + (P(),) * 13
    return jax.shard_map(
        on_device,
        mesh=mesh,
        in_specs=placed,
        out_specs=P(("grp", "seq"), "tok", None),
        check_vma=False,
    )
```

```python
import functools

import jax
import jax.numpy as jnp
from jax import lax
from jax.experimental import pallas as pl
from jax.experimental.pallas import tpu as pltpu
from jax.sharding import PartitionSpec as P


REL_MAX = 32
EPS = 1e-05
MASKED = -1000000000.0
DIRECT_MAX = 8
VMEM_GRANT = 20 << 20


F32 = jnp.float32
BF16 = jnp.bfloat16
VMEM = pl.BlockSpec(memory_space=pltpu.VMEM)
HBM = pl.BlockSpec(memory_space=pltpu.MemorySpace.HBM)


def column_of(row, size):
    here = lax.broadcasted_iota(jnp.int32, (size, size), 0) == lax.broadcasted_iota(
        jnp.int32, (size, size), 1
    )
    return jnp.sum(jnp.where(here, row, 0.0), axis=1, keepdims=True)


def factor_of(rows, mask_row, gain_col, weight_t):
    values = rows.astype(F32)
    mean = jnp.mean(values, axis=0, keepdims=True)
    centred = values - mean
    variance = jnp.mean(centred * centred, axis=0, keepdims=True)
    normed = (centred * lax.rsqrt(variance + EPS) * gain_col).astype(BF16)
    factor = jnp.dot(weight_t, normed, preferred_element_type=F32)
    return (factor * mask_row.astype(F32)).astype(BF16)


def load_all(pairs, sems):
    copies = [pltpu.make_async_copy(src, dst, sems.at[i]) for i, (src, dst) in enumerate(pairs)]
    for copy in copies:
        copy.start()
    return copies


def left_kernel(x_hbm, mask_hbm, gain_hbm, weight_hbm, out_ref, x_ref, mask_ref, gain_ref, weight_ref, sems):
    factor_dim = weight_ref.shape[0]
    rows = out_ref.shape[0] // factor_dim
    seq = lax.axis_index("seq")

    @pl.when(lax.axis_index("tok") == 0)
    def _():
        head = x_ref.shape[0]
        copies = load_all(
            [
                (gain_hbm, gain_ref),
                (weight_hbm, weight_ref),
                (mask_hbm.at[pl.ds(0, head)], mask_ref),
                (x_hbm.at[pl.ds(0, head)], x_ref),
            ],
            sems,
        )
        for copy in copies:
            copy.wait()
        gain_col = column_of(gain_ref[...], gain_ref.shape[1])
        weight_t = weight_ref[...]
        for i in range(rows):
            token = lax.rem(i + (1 - seq) * (rows // 2), rows)
            out_ref[pl.ds(i * factor_dim, factor_dim), :] = factor_of(
                x_ref[token], mask_ref[pl.ds(token, 1), :], gain_col, weight_t
            )


def payload_kernel(pair_hbm, res_hbm, chain_hbm, payload_ref, pair_ref, res_ref, chain_ref, sems):
    rows_dev, tokens_dev, channels = pair_ref.shape
    copies = load_all([(res_hbm, res_ref), (chain_hbm, chain_ref), (pair_hbm, pair_ref)], sems)
    for copy in copies:
        copy.wait()
    for r in range(rows_dev):
        payload_ref[pl.ds(r * tokens_dev, tokens_dev), :] = pair_ref[r]
    lane = lax.broadcasted_iota(jnp.int32, (tokens_dev, channels), 1)
    res_col = column_of(res_ref[...].astype(F32), tokens_dev)
    chain_col = column_of(chain_ref[...].astype(F32), tokens_dev)
    payload_ref[pl.ds(rows_dev * tokens_dev, tokens_dev), :] = jnp.where(
        lane < channels // 2, res_col, chain_col
    ).astype(BF16)


def right_kernel(x_ref, mask_ref, gain_ref, weight_ref, out_ref):
    factor_dim = weight_ref.shape[0]
    gain_col = column_of(gain_ref[...], gain_ref.shape[1])
    weight_t = weight_ref[...]
    for token in range(x_ref.shape[0]):
        out_ref[pl.ds(token * factor_dim, factor_dim), :] = factor_of(
            x_ref[token], mask_ref[pl.ds(token, 1), :], gain_col, weight_t
        )


def norm_lanes(values, gain_row):
    mean = jnp.mean(values, axis=1, keepdims=True)
    centred = values - mean
    variance = jnp.mean(centred * centred, axis=1, keepdims=True)
    return (centred * lax.rsqrt(variance + EPS) * gain_row).astype(BF16)


def attention_kernel(bits, *refs):
    (mask_ref, bias_ref, gain_ref, qg_ref, kv_ref, out_w_ref, rel_ref, opb_ref), refs = refs[:8], refs[8:]
    pieces, (out_ref, start_ref, code_ref) = refs[:-3], refs[-3:]
    rows_dev, width = mask_ref.shape
    heads, tokens_dev, _ = bias_ref.shape
    channels = gain_ref.shape[1]
    head_width = out_w_ref.shape[0]
    head_dim = head_width // heads
    rel_bins = rel_ref.shape[0]
    block = (rows_dev + 1) * tokens_dev
    tok, seq = lax.axis_index("tok"), lax.axis_index("seq")
    for k in range(width // tokens_dev):
        if bits:
            flip = sum(bit for i, bit in enumerate(bits) if k >> i & 1)
            level = k.bit_length()
            piece, base = pieces[level], (k - (1 << level >> 1)) * block
            where = jnp.bitwise_xor(tok, flip) * tokens_dev
            where = pl.multiple_of(where, tokens_dev)
        else:
            piece, base, where = pieces[0], k * block, k * tokens_dev
        for r in range(rows_dev):
            start_ref[r, pl.ds(where, tokens_dev), :] = piece[
                pl.ds(base + r * tokens_dev, tokens_dev), :
            ].astype(F32)
        code_ref[pl.ds(where, tokens_dev), :] = piece[
            pl.ds(base + rows_dev * tokens_dev, tokens_dev), :
        ].astype(F32)
    codes = code_ref[...]
    key_res = codes[:, :1]
    key_chain = codes[:, channels - 1 :]
    gain_row = gain_ref[...]
    classes = lax.broadcasted_iota(jnp.int32, (width, rel_bins), 1).astype(F32)
    own = pl.ds(pl.multiple_of(tok * tokens_dev, tokens_dev), tokens_dev)
    keys, values = [], []
    for r in range(rows_dev):
        row_code = code_ref[pl.ds(seq * rows_dev + r, 1), :]
        offset = jnp.clip(row_code[:, :1] - key_res + REL_MAX, 0, 2 * REL_MAX)
        rel_class = jnp.where(row_code[:, channels - 1 :] == key_chain, offset, 2 * REL_MAX + 1)
        onehot = jnp.where(classes == rel_class, 1.0, 0.0).astype(BF16)
        start = start_ref[r] + jnp.dot(onehot, rel_ref[...], preferred_element_type=F32)
        start_ref[r] = start
        normed = norm_lanes(start, gain_row)
        key_value = jnp.dot(normed, kv_ref[...], preferred_element_type=F32).astype(BF16)
        keys.append(key_value[:, :head_width])
        values.append(key_value[:, head_width:])
    mine = jnp.concatenate([start_ref[r, own, :] for r in range(rows_dev)], axis=0)
    query_gate = jnp.dot(norm_lanes(mine, gain_row), qg_ref[...], preferred_element_type=F32)
    query = query_gate[:, :head_width]
    gate = jax.nn.sigmoid(query_gate[:, head_width:])
    stacked = heads * tokens_dev
    bias = bias_ref[...].astype(F32).reshape(stacked, width)
    head_of_row = lax.broadcasted_iota(jnp.int32, (stacked, head_width), 0) // tokens_dev
    head_of_lane = lax.broadcasted_iota(jnp.int32, (stacked, head_width), 1) // head_dim
    same_head = head_of_row == head_of_lane
    mixed = []
    for r in range(rows_dev):
        query_r = query[r * tokens_dev : (r + 1) * tokens_dev]
        wide = jnp.where(same_head, jnp.concatenate([query_r] * heads, axis=0), 0.0).astype(BF16)
        logits = lax.dot_general(
            wide, keys[r], (((1,), (1,)), ((), ())), preferred_element_type=F32
        )
        logits = logits * head_dim ** (-0.5) + bias
        logits = jnp.where(mask_ref[r : r + 1, :] == 1, logits, MASKED)
        expo = jnp.exp(logits - jnp.max(logits, axis=1, keepdims=True))
        total = jnp.sum(expo, axis=1, keepdims=True)
        numer = jnp.dot(expo.astype(BF16), values[r], preferred_element_type=F32)
        picked = jnp.where(same_head, numer / total, 0.0)
        mixed.append(
            sum(picked[h * tokens_dev : (h + 1) * tokens_dev] for h in range(heads))
        )
    attended = (jnp.concatenate(mixed, axis=0) * gate).astype(BF16)
    update = jnp.dot(attended, out_w_ref[...], preferred_element_type=F32)
    out_ref[...] = mine + update + opb_ref[...]


def project(left_t, right_t, weight, count, scratch, factor_dim):
    rows = left_t.shape[0] // factor_dim
    tokens = right_t.shape[0] // factor_dim
    lanes = rows * factor_dim
    scratch[...] = lax.dot_general(
        right_t, left_t, (((1,), (1,)), ((), ())), preferred_element_type=F32
    ) * (1.0 / count)
    segment = lax.broadcasted_iota(jnp.int32, (tokens, lanes), 1) // factor_dim
    groups = [[] for _ in range(rows)]
    for group in range(factor_dim // rows):
        level = [scratch[pl.ds(group * rows + a, tokens, stride=factor_dim), :] for a in range(rows)]
        step = 1
        while step < rows:
            upper = (segment & step) != 0
            for low in range(rows):
                if low & step:
                    continue
                one, two = level[low], level[low + step]
                level[low] = jnp.where(upper, pltpu.roll(two, step * factor_dim, 1), one)
                level[low + step] = jnp.where(
                    upper, two, pltpu.roll(one, lanes - step * factor_dim, 1)
                )
            step *= 2
        for r in range(rows):
            groups[r].append(level[r])
    outer = jnp.concatenate([jnp.concatenate(g, axis=1) for g in groups], axis=0)
    high = outer.astype(BF16)
    low = (outer - high.astype(F32)).astype(BF16)
    return jnp.dot(high, weight, preferred_element_type=F32) + jnp.dot(
        low, weight, preferred_element_type=F32
    )


def pick(bit, rows, one_ref, two_ref):
    took = jnp.bitwise_and(lax.axis_index("tok"), bit) != 0
    return jnp.where(took, two_ref[rows, :], one_ref[rows, :])


def far_kernel(count, factor_dim, bit, left_ref, came_ref, right_ref, weight_ref, out_ref, scratch):
    left_t = pick(bit, pl.ds(0, left_ref.shape[0] // 2), left_ref, came_ref)
    out_ref[...] = project(left_t, right_ref[...], weight_ref[...], count, scratch, factor_dim).astype(
        BF16
    )


def near_kernel(count, factor_dim, bit, left_ref, came_ref, right_ref, weight_ref, mid_ref, out_ref, scratch):
    half = left_ref.shape[0] // 2
    left_t = pick(bit, pl.ds(half, half), left_ref, came_ref)
    out_ref[...] = mid_ref[...] + project(
        left_t, right_ref[...], weight_ref[...], count, scratch, factor_dim
    )


def transition_kernel(near_ref, other_ref, gain_ref, in_w_ref, out_w_ref, out_ref):
    after = near_ref[...] + other_ref[...].astype(F32)
    normed = norm_lanes(after, gain_ref[...])
    both = jnp.dot(normed, in_w_ref[...], preferred_element_type=F32)
    hidden_dim = out_w_ref.shape[0]
    up = both[:, :hidden_dim]
    hidden = (up * jax.nn.sigmoid(up) * both[:, hidden_dim:]).astype(BF16)
    update = jnp.dot(hidden, out_w_ref[...], preferred_element_type=F32)
    out_ref[...] = (after + update).astype(BF16)


def call(kernel, outs, specs, scratch=(), flops=0, **kw):
    one = not isinstance(outs, (list, tuple))
    return pl.pallas_call(
        kernel,
        out_shape=outs,
        in_specs=specs,
        out_specs=VMEM if one else [VMEM] * len(outs),
        scratch_shapes=scratch,
        cost_estimate=pl.CostEstimate(flops=flops, transcendentals=0, bytes_accessed=1 << 20),
        compiler_params=pltpu.CompilerParams(vmem_limit_bytes=VMEM_GRANT),
        **kw,
    )


def in_hbm(value):
    return pltpu.with_memory_space_constraint(value, pltpu.MemorySpace.HBM)


def join_kernel(one_ref, two_ref, out_ref):
    rows = one_ref.shape[0]
    out_ref[pl.ds(0, rows), :] = one_ref[...]
    out_ref[pl.ds(rows, rows), :] = two_ref[...]


def swap(value, axis, bit, size):
    return lax.ppermute(value, axis, [(i, i ^ bit) for i in range(size)])


def on_device(
    pair_slab_input,
    alignment_rows,
    alignment_row_mask,
    residue,
    chain,
    template_key_mask,
    triangle_head_bias,
    pair_attention_gain,
    query_gate_weight,
    key_value_weight,
    attention_output_weight,
    relative_position_weight,
    alignment_norm_gain,
    left_factor_weight,
    right_factor_weight,
    outer_product_weight,
    outer_product_bias,
    transition_gain,
    transition_input_weight,
    transition_output_weight,
):
    rows_dev, tokens_dev, channels = pair_slab_input.shape
    sequences = alignment_rows.shape[0]
    factor_dim = left_factor_weight.shape[1]
    size = lax.axis_size("tok")
    seqs = lax.axis_size("seq")
    count = sequences * seqs
    width = template_key_mask.shape[1]
    slab = rows_dev * seqs
    tok = lax.axis_index("tok")
    bits = [1 << k for k in range(size.bit_length() - 1)]
    tree = bits[:1] + bits[:0:-1]
    sds = jax.ShapeDtypeStruct
    flat = (rows_dev * tokens_dev, channels)

    rows_t = alignment_rows.transpose(1, 2, 0)
    mask_t = alignment_row_mask.T
    gain_row = alignment_norm_gain[None]
    first = -(-slab // 8) * 8
    scratch_of = lambda v, lead=None: pltpu.VMEM(((lead or v.shape[0]),) + v.shape[1:], v.dtype)
    left_in = (rows_t, mask_t, gain_row, left_factor_weight.T)
    first_left = call(
        left_kernel,
        sds((slab * factor_dim, sequences), BF16),
        [HBM] * 4,
        scratch=[scratch_of(v, f) for v, f in zip(left_in, (first, first, None, None))]
        + [pltpu.SemaphoreType.DMA((4,))],
    )(*[in_hbm(v) for v in left_in])
    pay_in = (pair_slab_input, residue[None], chain[None])
    payload = call(
        payload_kernel,
        sds(((rows_dev + 1) * tokens_dev, channels), BF16),
        [HBM] * 3,
        scratch=[scratch_of(v) for v in pay_in] + [pltpu.SemaphoreType.DMA((3,))],
    )(*[in_hbm(v) for v in pay_in])
    right_t = call(
        right_kernel, sds((tokens_dev * factor_dim, sequences), BF16), [VMEM] * 4, flops=1 << 29
    )(rows_t, mask_t, gain_row, right_factor_weight.T)

    order = bits[::-1] if size <= DIRECT_MAX else ()
    if order:
        pieces = [payload]
        held = payload
        for stage, bit in enumerate(order):
            if stage:
                joined = sds((2 * held.shape[0], channels), BF16)
                held = call(join_kernel, joined, [VMEM] * 2)(held, pieces[-1])
            pieces.append(swap(held, "tok", bit, size))
    else:
        pieces = [lax.all_gather(payload, "tok", axis=0, tiled=True)]

    came = held = first_left
    for stage, bit in enumerate(tree):
        if stage:
            held = jnp.where((tok & tree[stage - 1]) != 0, came, held)
        below = sum(tree[:stage])
        pairs = [(i, i ^ bit) for i in range(size) if i & ~below == 0]
        came = lax.ppermute(held, "tok", pairs)

    mid = call(
        functools.partial(attention_kernel, order),
        sds(flat, F32),
        [VMEM] * (8 + len(pieces)),
        scratch=[
            pltpu.VMEM((rows_dev, width, channels), F32),
            pltpu.VMEM((width, channels), F32),
        ],
        flops=1 << 30,
    )(
        template_key_mask, triangle_head_bias, pair_attention_gain[None], query_gate_weight, key_value_weight,
        attention_output_weight, relative_position_weight, outer_product_bias[None], *pieces,
    )

    weight = (
        outer_product_weight.reshape(factor_dim, factor_dim, channels)
        .transpose(1, 0, 2)
        .reshape(factor_dim * factor_dim, channels)
    )
    scratch = [pltpu.VMEM((tokens_dev * factor_dim, rows_dev * factor_dim), F32)]
    other = call(
        functools.partial(far_kernel, count, factor_dim, tree[-1]),
        sds(flat, BF16),
        [VMEM] * 4,
        scratch=scratch,
        flops=1 << 28,
    )(held, came, right_t, weight)
    other = swap(other, "seq", 1, seqs)
    near = call(
        functools.partial(near_kernel, count, factor_dim, tree[-1]),
        sds(flat, F32),
        [VMEM] * 5,
        scratch=scratch,
        flops=1 << 28,
    )(held, came, right_t, weight, mid)
    out = call(transition_kernel, sds(flat, BF16), [VMEM] * 5)(
        near, other, transition_gain[None], transition_input_weight, transition_output_weight
    )
    return out.reshape(rows_dev, tokens_dev, channels)


def solution(mesh):
    placed = (
        P(("grp", "seq"), "tok", None),
        P(("grp", "seq"), "tok", None),
        P(("grp", "seq"), "tok"),
        P(("grp", "tok")),
        P(("grp", "tok")),
        P(("grp", "seq"), None),
        P(None, ("grp", "tok"), None),
    ) + (P(),) * 13
    return jax.shard_map(
        on_device,
        mesh=mesh,
        in_specs=placed,
        out_specs=P(("grp", "seq"), "tok", None),
        check_vma=False,
    )
```
